32 devices in a mesh: ctx: 4 (over x, core), tp: 8 (over z, y).
Axes of the slice: x: 2, y: 2, z: 4, core: 2. Of those that a mesh axis runs over, the one named last changes fastest.
Arguments:
- token_ids: int32 [1024], replicated, may hold values from 0 to 128255
- doc_lengths: int32 [8], replicated, may hold values from 1 to 256, 1024 in all
- block_order: int32 [8], replicated, may hold values from 0 to 7, each once
- table: bfloat16 [128256, 8192], P('tp', 'ctx'), may hold values from -6 to 6
- gain: float32 [8192], replicated, may hold values from 0.5 to 12, as said below
- w_query: bfloat16 [8192, 8192], P('ctx', 'tp'), may hold values from -0.0625 to 0.0625
- w_keyval: bfloat16 [8192, 2, 1024], P('ctx'), may hold values from -0.0625 to 0.0625
Outputs:
- attended: bfloat16 [1024, 8192], P('ctx', 'tp')
The draws below stay inside these ranges and needn't reach their ends.
Inputs may be any that keep to these rules, and one draw needn't show every extreme that they name: `token_ids`: ids of the vocabulary. `doc_lengths`: the documents fill the slab in order, their lengths sum to 1024. `block_order`: a permutation of the 8 blocks of the slab. `gain`: positive gains.
All inputs are finite; a program needn't handle non-finite values.
Results may differ from the reference program's by a relative error of at most 0.007.
The reference program's roundings to bfloat16 on the way count: a program that leaves them out, or rounds other values in their place, can miss the bound.
Values may be sent and summed in bfloat16 or wider, within the bound.
A program may use at most 128 MiB of HBM per device.

```python
import math
import jax
import jax.numpy as jnp
import numpy as np
from jax import lax

VOCAB = 128256
D = 8192
HEADS = 64
KV_HEADS = 8
HD = 128
BLOCK = 128
TOKENS = 1024
BLOCKS = 8
DOCS = 8


def draw_gain(key, part):
    return jax.random.uniform(key, (D,), jnp.float32, minval=0.5, maxval=1.5)


def plant(entries, stream_key, least, high):
    place = [jax.random.randint(jax.random.fold_in(stream_key, axis), (), 0, length) for axis, length in enumerate(entries.shape)]
    longest = entries.shape.index(max(entries.shape))
    neighbour = place[:longest] + [(place[longest] + 1) % entries.shape[longest]] + place[longest + 1:]
    return entries.at[tuple(place)].set(least).at[tuple(neighbour)].set(high)


def steps_of(stream_key, dims, pieces, low, high):
    def one(axis_at, parts):
        draws = jax.random.uniform(jax.random.fold_in(jax.random.fold_in(stream_key, 6), axis_at), (parts,), jnp.float32, low / len(pieces), high / len(pieces))
        return jnp.repeat(jnp.exp(draws), dims[axis_at] // parts).reshape((-1,) + (1,) * (len(dims) - axis_at - 1))

    level = one(*pieces[0])
    for cut in pieces[1:]:
        level = level * one(*cut)
    return level


def skewed_wide(key, extent, number_of, lean):
    weights = [min(1 << octave, number_of + 1 - (1 << octave)) * (1 << 20) // math.isqrt((1 << octave) ** lean) + 1 for octave in range((number_of + 1).bit_length()) if 1 << octave <= number_of]
    scale = 1 + sum(weights) // (1 << 30)
    table = np.cumsum(np.array([max(1, weight // scale) for weight in weights]))
    lot = jax.random.randint(jax.random.fold_in(key, 1), extent, 0, int(table[len(weights) - 1]))
    start = jnp.left_shift(1, jnp.searchsorted(jnp.asarray(table, jnp.int32), lot, side="right").astype(jnp.int32))
    rank = start - 1 + jax.random.randint(jax.random.fold_in(key, 4), extent, 0, 1 << 30) % jnp.minimum(start, number_of + 1 - start)
    return jax.random.permutation(jax.random.fold_in(key, 2), number_of)[rank].astype(jnp.int32)


def split_up(count, total, most, lean):
    loads = [(1 << 20) // math.isqrt(rank ** lean) + 1 for rank in range(2, count + 1)]
    spare, given = total - most - (count - 1), [1] * (count - 1)
    while spare > 0:
        candidates = [i for i in range(count - 1) if given[i] < most]
        mass, remaining = sum([loads[i] for i in candidates]), spare
        for i in candidates:
            addition = min(most - given[i], max(1, remaining * loads[i] // mass), spare)
            given[i] = given[i] + addition
            spare = spare - addition
    return np.array([most] + given)


def ragged(rng, amount, total, limit, lean):
    if amount == 2:
        one = jax.random.randint(rng, (), max(1, total - limit), min(limit, total - 1) + 1)
        return jnp.stack([one, total - one])
    tallies = jnp.asarray(split_up(amount, total, limit, lean), jnp.int32)
    couples = (amount - 1) // 2
    giver, taker = tallies[1:1 + 2 * couples:2], tallies[2:2 + 2 * couples:2]
    room = jnp.minimum(giver - 1, limit - taker)
    shifted = jax.random.randint(jax.random.fold_in(rng, 1), (couples,), 0, 1 << 20) % (room + 1)
    tallies = tallies.at[1:1 + 2 * couples:2].set(giver - shifted).at[2:2 + 2 * couples:2].set(taker + shifted)
    return tallies[jax.random.permutation(jax.random.fold_in(rng, 2), amount)]


def noise(stream_key, extent, spread, limit, split=(), kind=jnp.bfloat16):
    values = jax.random.normal(stream_key, extent, jnp.float32) * spread
    if len(split) > 0:
        values = steps_of(stream_key, extent, split, -0.22, 0.18) * values
    return jnp.clip(values, min=-limit, max=limit).astype(kind)


def setup_inputs(seed: int = 0) -> dict:
    arg_keys = jax.random.split(jax.random.key(seed), 8)
    token_ids = plant(skewed_wide(arg_keys[0], (TOKENS,), VOCAB, 2), jax.random.fold_in(arg_keys[0], 3), 0, VOCAB - 1).astype(jnp.int32)
    doc_lengths = ragged(arg_keys[1], DOCS, TOKENS, TOKENS // 4, 2).astype(jnp.int32)
    block_order = jax.random.permutation(arg_keys[2], BLOCKS).astype(jnp.int32)
    table = noise(arg_keys[3], (VOCAB, D), 1.0, 6.0, ((0, 8), (1, 4)))
    gain = draw_gain(jax.random.fold_in(arg_keys[7], 71), 0)
    w_query = noise(arg_keys[5], (D, HEADS * HD), D ** -0.5, 0.0625, ((0, 4), (1, 8)))
    w_keyval = noise(arg_keys[6], (D, 2, KV_HEADS * HD), D ** -0.5, 0.0625, ((0, 4),))
    return {"token_ids": token_ids, "doc_lengths": doc_lengths, "block_order": block_order, "table": table, "gain": gain, "w_query": w_query, "w_keyval": w_keyval}


rotary_base = 500000.0

def rotary(values_in, pos_rows):
    half_dim = values_in.shape[-1] // 2
    steps_up = jnp.arange(half_dim, dtype=jnp.float32)
    freqs = jnp.power(rotary_base, -2.0 * steps_up / values_in.shape[-1])
    angle = pos_rows.astype(jnp.float32)[:, None] * freqs[None, :]
    angle = angle.reshape((angle.shape[0],) + (1,) * (values_in.ndim - 2) + (half_dim,))
    cosine = jnp.cos(angle)
    sine = jnp.sin(angle)
    first = values_in[..., :half_dim]
    second = values_in[..., half_dim:]
    return jnp.concatenate([first * cosine - second * sine, second * cosine + first * sine], axis=-1)

def document_of(pos_rows, doc_lengths):
    ends = jnp.cumsum(doc_lengths).astype(jnp.int32)
    return lax.optimization_barrier(jnp.sum((ends[None, :] <= pos_rows[:, None]).astype(jnp.int32), axis=1)).astype(jnp.int32)

def reference(token_ids, doc_lengths, block_order, table, gain, w_query, w_keyval):
    row_index = jnp.arange(TOKENS, dtype=jnp.int32)
    positions = (block_order[row_index // BLOCK] * BLOCK + row_index % BLOCK).astype(jnp.int32)
    embed = table[token_ids[positions]]
    embed32 = embed.astype(jnp.float32)
    inverse = lax.rsqrt(lax.optimization_barrier(jnp.mean(embed32 * embed32, axis=1)) + 1e-05)
    scaled = (embed32 * gain).astype(jnp.bfloat16)
    query_raw = jnp.dot(scaled, w_query, preferred_element_type=jnp.float32) * inverse[:, None]
    queries = rotary(query_raw.reshape(TOKENS, HEADS, HD), positions).astype(jnp.bfloat16)
    key_raw = jnp.dot(scaled, w_keyval[:, 0, :], preferred_element_type=jnp.float32) * inverse[:, None]
    keys = rotary(key_raw.reshape(TOKENS, KV_HEADS, HD), positions).astype(jnp.bfloat16)
    value_raw = jnp.dot(scaled, w_keyval[:, 1, :], preferred_element_type=jnp.float32) * inverse[:, None]
    values = value_raw.reshape(TOKENS, KV_HEADS, HD).astype(jnp.bfloat16)
    document = document_of(positions, doc_lengths)
    allowed = (document[None, :] == document[:, None]) & (positions[None, :] <= positions[:, None])
    group = HEADS // KV_HEADS

    def one_head(head_at):
        query_head = queries[:, head_at, :]
        key_head = keys[:, head_at // group, :]
        value_head = values[:, head_at // group, :]
        scores = jnp.dot(query_head, key_head.T, preferred_element_type=jnp.float32) / jnp.sqrt(jnp.float32(HD))
        masked = jnp.where(allowed, scores, jnp.float32(-1e+30))
        largest = lax.optimization_barrier(jnp.max(masked, axis=1))
        weights = jnp.where(allowed, jnp.exp(masked - largest[:, None]), jnp.float32(0.0))
        totals = lax.optimization_barrier(jnp.sum(weights, axis=1))
        mixed = jnp.dot(weights.astype(jnp.bfloat16), value_head, preferred_element_type=jnp.float32)
        return (mixed / totals[:, None]).astype(jnp.bfloat16)
    per_head = lax.map(one_head, jnp.arange(HEADS, dtype=jnp.int32))
    return jnp.transpose(per_head, (1, 0, 2)).reshape(TOKENS, HEADS * HD)
```

```python
import functools

import jax
import jax.numpy as jnp
from jax import lax
from jax.experimental import pallas as pl
from jax.experimental.pallas import tpu as pltpu
from jax.sharding import PartitionSpec as P

HEADS = 64
KV_HEADS = 8
HD = 128
BLOCK = 128
GROUP_ROWS = 8
MESH = pl.DeviceIdType.MESH
VMEM_SPEC = pl.BlockSpec(memory_space=pltpu.VMEM)
VMEM_LIMIT = 60 * 1024 * 1024


rotary_base = 500000.0


def greet(axis, others):
    barrier = pltpu.get_barrier_semaphore()
    for other in others:
        pl.semaphore_signal(barrier, inc=1, device_id={axis: other}, device_id_type=MESH)
    pl.semaphore_wait(barrier, len(others))


def pick_kernel(group_ref, table_ref, lane_ref, out_ref, held, sem):
    count = out_ref.shape[0]

    @pl.loop(0, count, unroll=8)
    def _(k):
        source = pl.multiple_of(group_ref[k] * GROUP_ROWS, GROUP_ROWS)
        target = pl.multiple_of(k * GROUP_ROWS, GROUP_ROWS)
        pltpu.make_async_copy(
            table_ref.at[pl.ds(source, GROUP_ROWS)], held.at[pl.ds(target, GROUP_ROWS)], sem
        ).start()

    pltpu.make_async_copy(table_ref.at[pl.ds(0, count * GROUP_ROWS)], held, sem).wait()
    tile = min(count, 128)
    for at in range(0, count, tile):
        row = lax.broadcasted_iota(jnp.int32, (tile, tile * GROUP_ROWS), 0) * GROUP_ROWS
        column = lax.broadcasted_iota(jnp.int32, (tile, tile * GROUP_ROWS), 1)
        choose = (column == row + lane_ref[at : at + tile, :1]).astype(jnp.float32).astype(jnp.bfloat16)
        out_ref[at : at + tile] = jnp.dot(
            choose,
            held[at * GROUP_ROWS : (at + tile) * GROUP_ROWS],
            preferred_element_type=jnp.float32,
        ).astype(out_ref.dtype)


def pick_rows(table, local_ids):
    count = local_ids.shape[0]
    columns = table.shape[1]
    lane = jnp.broadcast_to((local_ids % GROUP_ROWS)[:, None], (count, 128))
    return pl.pallas_call(
        pick_kernel,
        out_shape=jax.ShapeDtypeStruct((count, columns), table.dtype),
        grid_spec=pltpu.PrefetchScalarGridSpec(
            num_scalar_prefetch=1,
            grid=(),
            in_specs=[pl.BlockSpec(memory_space=pl.ANY), VMEM_SPEC],
            out_specs=VMEM_SPEC,
            scratch_shapes=[
                pltpu.VMEM((count * GROUP_ROWS, columns), table.dtype),
                pltpu.SemaphoreType.DMA,
            ],
        ),
    )(local_ids // GROUP_ROWS, table, lane)


def spread_kernel(ring, x_ref, out_ref, own_sem, send_sem, recv_sem):
    me = lax.axis_index("tp")
    at, side = me // 2, lax.rem(me, 2)
    up = lax.rem(at + 1, ring) * 2 + side
    down = lax.rem(at + ring - 1, ring) * 2 + side
    across = at * 2 + 1 - side
    greet("tp", (up, down, across))
    part = x_ref.shape[0] // 4
    last = ring - 1
    own = pltpu.make_async_copy(x_ref, out_ref.at[me], own_sem)
    own.start()
    sends = []

    def slot(back, other, q):
        origin = lax.rem(at + ring - back, ring) * 2 + (1 - side if other else side)
        return out_ref.at[origin, pl.ds(q * part, part)]

    def copy(back, other, q, way):
        here = slot(back, other, q)
        source = x_ref.at[pl.ds(q * part, part)] if (back, other) == (0, 0) else here
        target = {"up": up, "down": down, "across": across}[way]
        lands = {
            "up": ((back + 1) % ring, other),
            "down": ((back + last) % ring, other),
            "across": (back, 1 - other),
        }[way]
        number = len(sends)
        sent = pltpu.make_async_remote_copy(
            src_ref=source,
            dst_ref=here,
            send_sem=send_sem.at[number],
            recv_sem=recv_sem.at[lands[0] * 2 + lands[1], q],
            device_id={"tp": target},
            device_id_type=MESH,
        )
        sent.start()
        sends.append(sent)

    seen = set()

    def arrive(back, other, q):
        seen.add((back, other, q))
        here = slot(back, other, q)
        pltpu.make_async_copy(here, here, recv_sem.at[back * 2 + other, q]).wait()

    for q in (0, 1):
        copy(0, 0, q, "across")
    for q in (2, 3):
        copy(0, 0, q, "up")
        copy(0, 0, 5 - q, "down")
    for q in (0, 1):
        copy(0, 0, q, "up")
        copy(0, 0, 1 - q, "down")
    for q in (2, 3):
        copy(0, 0, q, "across")
    arrive(0, 1, 0)
    copy(0, 1, 0, "up")
    copy(0, 1, 0, "down")
    arrive(1, 0, 2)
    copy(1, 0, 2, "up")
    copy(1, 0, 2, "across")
    arrive(last, 0, 3)
    copy(last, 0, 3, "down")
    copy(last, 0, 3, "across")
    arrive(0, 1, 1)
    copy(0, 1, 1, "up")
    copy(0, 1, 1, "down")
    arrive(1, 0, 3)
    copy(1, 0, 3, "across")
    arrive(last, 0, 2)
    copy(last, 0, 2, "across")
    arrive(1, 0, 0)
    copy(1, 0, 0, "up")
    arrive(last, 0, 1)
    copy(last, 0, 1, "down")
    for q in (2, 3):
        arrive(2, 0, q)
        copy(2, 0, q, "across")
    arrive(1, 1, 0)
    copy(1, 1, 0, "up")
    arrive(last, 1, 1)
    copy(last, 1, 1, "down")
    for back in range(ring):
        for other in (0, 1):
            for q in range(4):
                if (back, other) != (0, 0) and (back, other, q) not in seen:
                    arrive(back, other, q)
    own.wait()
    for sent in sends:
        sent.wait_send()


def spread(rows, collective_id):
    tp_count = lax.axis_size("tp")
    count, columns = rows.shape
    ring = tp_count // 2
    if ring != 4 or count % 64:
        return lax.all_gather(rows, "tp", axis=0, tiled=True)
    out = pl.pallas_call(
        functools.partial(spread_kernel, ring),
        out_shape=jax.ShapeDtypeStruct((tp_count, count, columns), rows.dtype),
        in_specs=[VMEM_SPEC],
        out_specs=VMEM_SPEC,
        scratch_shapes=[
            pltpu.SemaphoreType.DMA,
            pltpu.SemaphoreType.DMA((28,)),
            pltpu.SemaphoreType.DMA((tp_count, 4)),
        ],
        compiler_params=pltpu.CompilerParams(
            collective_id=collective_id, has_side_effects=True, vmem_limit_bytes=VMEM_LIMIT
        ),
    )(rows)
    return out.reshape(tp_count * count, columns)


def fold_kernel(n, pieces, arrays, *refs):
    parts, outs = refs[:arrays], refs[arrays : 2 * arrays]
    near, far = refs[2 * arrays : 3 * arrays], refs[3 * arrays : 4 * arrays]
    near_send, near_recv, far_send, far_recv = refs[4 * arrays :]
    chips = n // 2
    me = lax.axis_index("ctx")
    chip, core = me // 2, lax.rem(me, 2)
    mate = chip * 2 + 1 - core
    remote = [lax.rem(chip + step, chips) * 2 + core for step in range(1, chips)]
    greet("ctx", [mate] + remote)
    sends = []

    def give(index, step):
        which, low, size = pieces[index]
        target = lax.rem(chip + step, chips) * 2 + 1 - core
        sent = pltpu.make_async_remote_copy(
            src_ref=parts[which].at[target, pl.ds(low, size)],
            dst_ref=near[which].at[step, pl.ds(low, size)],
            send_sem=near_send.at[index, step],
            recv_sem=near_recv.at[index, step],
            device_id={"ctx": mate},
            device_id_type=MESH,
        )
        sent.start()
        sends.append(sent)
        return sent

    handed = {}
    for step in list(range(1, chips)) + [0]:
        for index in range(len(pieces)):
            handed[index, step] = give(index, step)
    crossed = {}
    for index, (which, low, size) in enumerate(pieces):
        rows = pl.ds(low, size)
        for step in range(1, chips):
            target = remote[step - 1]
            handed[index, step].wait_recv()
            near[which][step, rows] = near[which][step, rows] + parts[which][target, rows]
            sent = pltpu.make_async_remote_copy(
                src_ref=near[which].at[step, rows],
                dst_ref=far[which].at[step, rows],
                send_sem=far_send.at[index, step],
                recv_sem=far_recv.at[index, step],
                device_id={"ctx": target},
                device_id_type=MESH,
            )
            sent.start()
            sends.append(sent)
            crossed[index, step] = sent
    for index, (which, low, size) in enumerate(pieces):
        rows = pl.ds(low, size)
        handed[index, 0].wait_recv()
        total = parts[which][me, rows] + near[which][0, rows]
        for step in range(1, chips):
            crossed[index, step].wait_recv()
            total = total + far[which][step, rows]
        outs[which][rows] = total
    for sent in sends:
        sent.wait_send()


def fold(*arrays):
    n = arrays[0].shape[0]
    chips = n // 2
    pieces = []
    for which, array in enumerate(arrays):
        size = array.shape[1]
        cut = size // 4 if size * array.shape[2] > 131072 else size
        pieces += [(which, low, cut) for low in range(0, size, cut)]
    sems = pltpu.SemaphoreType.DMA((len(pieces), chips))
    slots = [pltpu.VMEM((chips,) + a.shape[1:], a.dtype) for a in arrays]
    return pl.pallas_call(
        functools.partial(fold_kernel, n, tuple(pieces), len(arrays)),
        out_shape=[jax.ShapeDtypeStruct(a.shape[1:], a.dtype) for a in arrays],
        in_specs=[VMEM_SPEC] * len(arrays),
        out_specs=[VMEM_SPEC] * len(arrays),
        scratch_shapes=slots + slots + [sems] * 4,
        compiler_params=pltpu.CompilerParams(
            collective_id=2, has_side_effects=True, vmem_limit_bytes=VMEM_LIMIT
        ),
    )(*arrays)


def share_kernel(n, x_ref, out_ref, own_sem, send_sem, recv_sem):
    me = lax.axis_index("ctx")
    greet("ctx", [lax.rem(me + step, n) for step in range(1, n)])
    own = pltpu.make_async_copy(x_ref, out_ref.at[me], own_sem)
    own.start()
    copies = []
    for step in range(1, n):
        copy = pltpu.make_async_remote_copy(
            src_ref=x_ref,
            dst_ref=out_ref.at[me],
            send_sem=send_sem.at[step],
            recv_sem=recv_sem.at[step],
            device_id={"ctx": lax.rem(me + step, n)},
            device_id_type=MESH,
        )
        copy.start()
        copies.append(copy)
    for step in range(1, n):
        lands = out_ref.at[lax.rem(me + n - step, n)]
        pltpu.make_async_copy(lands, lands, recv_sem.at[step]).wait()
    own.wait()
    for copy in copies:
        copy.wait_send()


def share(rows):
    n = lax.axis_size("ctx")
    out = pl.pallas_call(
        functools.partial(share_kernel, n),
        out_shape=jax.ShapeDtypeStruct((n,) + rows.shape, rows.dtype),
        in_specs=[VMEM_SPEC],
        out_specs=VMEM_SPEC,
        scratch_shapes=[
            pltpu.SemaphoreType.DMA,
            pltpu.SemaphoreType.DMA((n,)),
            pltpu.SemaphoreType.DMA((n,)),
        ],
        compiler_params=pltpu.CompilerParams(collective_id=3, has_side_effects=True),
    )(rows)
    return out.reshape(n * rows.shape[0], rows.shape[1])


def rotary(values_in, pos_rows):
    half_dim = values_in.shape[-1] // 2
    steps_up = jnp.arange(half_dim, dtype=jnp.float32)
    freqs = jnp.power(rotary_base, -2.0 * steps_up / values_in.shape[-1])
    angle = pos_rows.astype(jnp.float32)[:, None] * freqs[None, :]
    angle = angle.reshape((angle.shape[0],) + (1,) * (values_in.ndim - 2) + (half_dim,))
    cosine = jnp.cos(angle)
    sine = jnp.sin(angle)
    first = values_in[..., :half_dim]
    second = values_in[..., half_dim:]
    return jnp.concatenate(
        [first * cosine - second * sine, second * cosine + first * sine], axis=-1
    )


def document_of(pos_rows, doc_lengths):
    ends = jnp.cumsum(doc_lengths)
    return jnp.sum((ends[None, :] <= pos_rows[:, None]).astype(jnp.int32), axis=1)


def plan(token_ids, vocab_here, capacity):
    tokens_all = token_ids.shape[0]
    order = jnp.arange(tokens_all, dtype=jnp.int32)
    same = token_ids[:, None] == token_ids[None, :]
    first = jnp.min(jnp.where(same, order[None, :], tokens_all), axis=1)
    shard = token_ids // vocab_here
    leads = first == order
    before = (order[None, :] < first[:, None]) & leads[None, :] & (shard[None, :] == shard[:, None])
    rank = jnp.sum(before.astype(jnp.int32), axis=1)
    most = jnp.max(rank) + 1
    return shard, rank, leads, (most + capacity - 1) // capacity


def shards(token_ids, doc_lengths, block_order, table, gain, w_query, w_keyval):
    ctx_count = lax.axis_size("ctx")
    ctx_at = lax.axis_index("ctx")
    tp_count = lax.axis_size("tp")
    tp_at = lax.axis_index("tp")
    tokens_all = token_ids.shape[0]
    tok_here = tokens_all // ctx_count
    vocab_here = table.shape[0]
    columns = table.shape[1]
    width = gain.shape[0]
    heads_here = HEADS // tp_count
    blocks = tokens_all // BLOCK
    capacity = tokens_all // tp_count
    positions = (
        block_order[:, None] * BLOCK + jnp.arange(BLOCK, dtype=jnp.int32)[None, :]
    ).reshape(tokens_all)

    def redeal(values):
        pick = block_order[:, None] == jnp.arange(blocks, dtype=jnp.int32)[None, :]
        spread_out = jnp.where(pick[:, :, None], values.reshape(1, blocks, BLOCK), 0)
        return jnp.sum(spread_out, axis=1).reshape(tokens_all)

    shard, rank, leads, rounds = plan(token_ids, vocab_here, capacity)
    local_ids = token_ids - tp_at * vocab_here
    mine = leads & (shard == tp_at)
    row_shard, row_rank = redeal(shard), redeal(rank)

    def one_round(number, collective_id):
        wanted = number * capacity + jnp.arange(capacity, dtype=jnp.int32)
        hit = mine[None, :] & (rank[None, :] == wanted[:, None])
        asked = jnp.sum(jnp.where(hit, local_ids[None, :], 0), axis=1)
        gathered = spread(pick_rows(table, asked), collective_id)
        in_round = (row_rank >= number * capacity) & (row_rank < (number + 1) * capacity)
        slot = jnp.where(in_round, row_shard * capacity + row_rank - number * capacity, -1)
        choose = slot[:, None] == jnp.arange(tp_count * capacity, dtype=jnp.int32)[None, :]
        return jnp.dot(
            choose.astype(table.dtype), gathered, preferred_element_type=jnp.float32
        ).astype(table.dtype)

    embed = one_round(0, 0)
    embed = lax.fori_loop(1, rounds, lambda i, held: held + one_round(i, 1), embed)
    col_embed = embed.astype(jnp.float32)
    kv_head = tp_at * heads_here // (HEADS // KV_HEADS)
    w_pair = lax.dynamic_slice_in_dim(w_keyval, kv_head * HD, HD, 2).reshape(
        w_keyval.shape[0], 2 * HD
    )
    gain_here = lax.dynamic_slice_in_dim(gain, ctx_at * columns, columns)
    col_scaled = (col_embed * gain_here).astype(jnp.bfloat16)
    query_term = jnp.dot(col_scaled, w_query, preferred_element_type=jnp.float32)
    pair_term = jnp.dot(col_scaled, w_pair, preferred_element_type=jnp.float32)
    square_term = jnp.sum(col_embed * col_embed, axis=1)
    pair_raw, query_raw, sumsq = fold(
        pair_term.reshape(ctx_count, tok_here, 2 * HD),
        query_term.reshape(ctx_count, tok_here, heads_here * HD),
        jnp.broadcast_to(square_term.reshape(ctx_count, 1, tok_here), (ctx_count, 8, tok_here)),
    )
    inverse = lax.rsqrt(sumsq[0] / width + 1e-05)
    my_pos = lax.dynamic_slice_in_dim(positions, ctx_at * tok_here, tok_here)
    query_rows = rotary(
        (query_raw * inverse[:, None]).reshape(tok_here, heads_here, HD), my_pos
    ).astype(jnp.bfloat16)
    key_rows = rotary(pair_raw[:, :HD] * inverse[:, None], my_pos).astype(jnp.bfloat16)
    value_rows = (pair_raw[:, HD:] * inverse[:, None]).astype(jnp.bfloat16)
    my_doc = document_of(my_pos, doc_lengths)
    stacked = jnp.transpose(query_rows, (1, 0, 2)).reshape(heads_here * tok_here, HD)
    query_pos = jnp.tile(my_pos, heads_here)
    query_doc = jnp.tile(my_doc, heads_here)
    inv_root = 1.0 / jnp.sqrt(jnp.float32(HD))
    shared = share(jnp.concatenate([key_rows, value_rows], axis=1))
    key_piece, value_piece = shared[:, :HD], shared[:, HD:]
    key_doc = document_of(positions, doc_lengths)
    allowed = (key_doc[None, :] == query_doc[:, None]) & (positions[None, :] <= query_pos[:, None])
    scores = (
        lax.dot_general(
            stacked, key_piece, (((1,), (1,)), ((), ())), preferred_element_type=jnp.float32
        )
        * inv_root
    )
    masked = jnp.where(allowed, scores, jnp.float32(-1e30))
    largest = jnp.max(masked, axis=1)
    weights = jnp.where(allowed, jnp.exp(masked - largest[:, None]), jnp.float32(0.0))
    totals = jnp.sum(weights, axis=1)
    accum = jnp.dot(weights.astype(jnp.bfloat16), value_piece, preferred_element_type=jnp.float32)
    mixed = (accum / totals[:, None]).reshape(heads_here, tok_here, HD)
    return jnp.transpose(mixed, (1, 0, 2)).reshape(tok_here, heads_here * HD).astype(jnp.bfloat16)


def solution(mesh):
    in_specs = (P(), P(), P(), P("tp", "ctx"), P(), P("ctx", "tp"), P("ctx", None, None))
    out_specs = P("ctx", "tp")
    return jax.shard_map(shards, mesh=mesh, in_specs=in_specs, out_specs=out_specs, check_vma=False)
```

```python
import functools

import jax
import jax.numpy as jnp
from jax import lax
from jax.experimental import pallas as pl
from jax.experimental.pallas import tpu as pltpu
from jax.sharding import PartitionSpec as P

HEADS = 64
KV_HEADS = 8
HD = 128
BLOCK = 128
GROUP_ROWS = 8
MESH = pl.DeviceIdType.MESH
VMEM_SPEC = pl.BlockSpec(memory_space=pltpu.VMEM)
VMEM_LIMIT = 60 * 1024 * 1024


rotary_base = 500000.0


def greet(axis, others):
    barrier = pltpu.get_barrier_semaphore()
    for other in others:
        pl.semaphore_signal(barrier, inc=1, device_id={axis: other}, device_id_type=MESH)
    pl.semaphore_wait(barrier, len(others))


def pick_kernel(group_ref, table_ref, lane_ref, out_ref, held, sem):
    count = out_ref.shape[0]

    @pl.loop(0, count, unroll=8)
    def _(k):
        source = pl.multiple_of(group_ref[k] * GROUP_ROWS, GROUP_ROWS)
        target = pl.multiple_of(k * GROUP_ROWS, GROUP_ROWS)
        pltpu.make_async_copy(
            table_ref.at[pl.ds(source, GROUP_ROWS)], held.at[pl.ds(target, GROUP_ROWS)], sem
        ).start()

    pltpu.make_async_copy(table_ref.at[pl.ds(0, count * GROUP_ROWS)], held, sem).wait()
    tile = min(count, 128)
    for at in range(0, count, tile):
        row = lax.broadcasted_iota(jnp.int32, (tile, tile * GROUP_ROWS), 0) * GROUP_ROWS
        column = lax.broadcasted_iota(jnp.int32, (tile, tile * GROUP_ROWS), 1)
        choose = (column == row + lane_ref[at : at + tile, :1]).astype(jnp.float32).astype(jnp.bfloat16)
        out_ref[at : at + tile] = jnp.dot(
            choose,
            held[at * GROUP_ROWS : (at + tile) * GROUP_ROWS],
            preferred_element_type=jnp.float32,
        ).astype(out_ref.dtype)


def pick_rows(table, local_ids):
    count = local_ids.shape[0]
    columns = table.shape[1]
    lane = jnp.broadcast_to((local_ids % GROUP_ROWS)[:, None], (count, 128))
    return pl.pallas_call(
        pick_kernel,
        out_shape=jax.ShapeDtypeStruct((count, columns), table.dtype),
        grid_spec=pltpu.PrefetchScalarGridSpec(
            num_scalar_prefetch=1,
            grid=(),
            in_specs=[pl.BlockSpec(memory_space=pl.ANY), VMEM_SPEC],
            out_specs=VMEM_SPEC,
            scratch_shapes=[
                pltpu.VMEM((count * GROUP_ROWS, columns), table.dtype),
                pltpu.SemaphoreType.DMA,
            ],
        ),
    )(local_ids // GROUP_ROWS, table, lane)


def spread_kernel(line, x_ref, out_ref, own_sem, send_sem, recv_sem):
    me = lax.axis_index("tp")
    at, side = me // 2, lax.rem(me, 2)
    last = line - 1
    up = jnp.minimum(at + 1, last) * 2 + side
    down = jnp.maximum(at - 1, 0) * 2 + side
    across = at * 2 + 1 - side
    barrier = pltpu.get_barrier_semaphore()

    def hail(other):
        pl.semaphore_signal(barrier, inc=1, device_id={"tp": other}, device_id_type=MESH)

    hail(across)
    pl.when(at < last)(lambda: hail(up))
    pl.when(at > 0)(lambda: hail(down))
    inner = (at > 0) & (at < last)
    pl.when(inner)(lambda: pl.semaphore_wait(barrier, 3))
    pl.when(jnp.logical_not(inner))(lambda: pl.semaphore_wait(barrier, 2))

    unit = x_ref.shape[0] // 8
    pieces = [(0, 1), (1, 2), (3, 2), (5, 2), (7, 1)]
    pair_first, line_first = (0, 1), (2, 3, 4)
    own = pltpu.make_async_copy(x_ref, out_ref.at[me], own_sem)
    own.start()
    sends = []

    def view(ref, q):
        low, size = pieces[q]
        return ref.at[pl.ds(low * unit, size * unit)]

    def start(origin, q, way, condition, mine=False):
        target = {"up": up, "down": down, "across": across}[way]
        copy = pltpu.make_async_remote_copy(
            src_ref=view(x_ref if mine else out_ref.at[origin], q),
            dst_ref=view(out_ref.at[origin], q),
            send_sem=send_sem.at[len(sends)],
            recv_sem=recv_sem.at[origin, q],
            device_id={"tp": target},
            device_id_type=MESH,
        )
        sends.append((condition, copy))
        if condition is None:
            copy.start()
        else:
            pl.when(condition)(copy.start)

    def arrive(origin, q, condition):
        here = view(out_ref.at[origin], q)
        wait = pltpu.make_async_copy(here, here, recv_sem.at[origin, q]).wait
        if condition is None:
            wait()
        else:
            pl.when(condition)(wait)

    for q in pair_first:
        start(me, q, "across", None, True)
    for q in line_first + pair_first:
        start(me, q, "up", at < last, True)
        start(me, q, "down", at > 0, True)
    for q in line_first:
        start(me, q, "across", None, True)

    def along(step, q, other, cross):
        half = 1 - side if other else side
        lower = jnp.maximum(at - step, 0) * 2 + half
        upper = jnp.minimum(at + step, last) * 2 + half
        arrive(lower, q, at >= step)
        if step < last:
            start(lower, q, "up", (at >= step) & (at < last))
        if cross:
            start(lower, q, "across", at >= step)
        arrive(upper, q, at <= last - step)
        if step < last:
            start(upper, q, "down", (at <= last - step) & (at > 0))
        if cross:
            start(upper, q, "across", at <= last - step)

    for step in range(1, line):
        if step == 1:
            for q in pair_first:
                arrive(across, q, None)
                start(across, q, "up", at < last)
                start(across, q, "down", at > 0)
        for q in line_first:
            along(step, q, 0, True)
        for q in pair_first:
            along(step, q, 0, False)
        for q in pair_first:
            along(step, q, 1, False)
    for q in line_first:
        for place in range(line):
            arrive(place * 2 + 1 - side, q, None)
    own.wait()
    for condition, copy in sends:
        if condition is None:
            copy.wait_send()
        else:
            pl.when(condition)(copy.wait_send)


def spread(rows, collective_id):
    tp_count = lax.axis_size("tp")
    count, columns = rows.shape
    line = tp_count // 2
    if line != 4 or count % 128:
        return lax.all_gather(rows, "tp", axis=0, tiled=True)
    out = pl.pallas_call(
        functools.partial(spread_kernel, line),
        out_shape=jax.ShapeDtypeStruct((tp_count, count, columns), rows.dtype),
        in_specs=[VMEM_SPEC],
        out_specs=VMEM_SPEC,
        scratch_shapes=[
            pltpu.SemaphoreType.DMA,
            pltpu.SemaphoreType.DMA((80,)),
            pltpu.SemaphoreType.DMA((tp_count, 5)),
        ],
        compiler_params=pltpu.CompilerParams(
            collective_id=collective_id, has_side_effects=True, vmem_limit_bytes=VMEM_LIMIT
        ),
    )(rows)
    return out.reshape(tp_count * count, columns)


def project_kernel(slot_ref, rows_ref, gain_ref, wq_ref, wp_ref, q_ref, p_ref, sq_ref, choose, squares):
    step = pl.program_id(1)
    total, slots = choose.shape
    sub = min(total, 512)

    @pl.when(step == 0)
    def _():
        q_ref[...] = jnp.zeros_like(q_ref)
        p_ref[...] = jnp.zeros_like(p_ref)
        squares[...] = jnp.zeros_like(squares)

        @pl.loop(0, total // 128)
        def _(r):
            rows = pl.ds(pl.multiple_of(r * 128, 128), 128)
            place = lax.broadcasted_iota(jnp.int32, (128, slots), 1)
            choose[rows] = (place == slot_ref[rows, :1]).astype(jnp.float32).astype(choose.dtype)

    @pl.loop(0, total // sub)
    def _(r):
        rows = pl.ds(pl.multiple_of(r * sub, sub), sub)
        embed = jnp.dot(choose[rows], rows_ref[...], preferred_element_type=jnp.float32)
        square = embed * embed
        folded = square[:, :128]
        for lane in range(128, square.shape[1], 128):
            folded = folded + square[:, lane : lane + 128]
        squares[rows] = squares[rows] + folded
        scaled = (embed * gain_ref[...]).astype(jnp.bfloat16)
        q_ref[rows] = q_ref[rows] + jnp.dot(scaled, wq_ref[...], preferred_element_type=jnp.float32)
        p_ref[rows] = p_ref[rows] + jnp.dot(scaled, wp_ref[...], preferred_element_type=jnp.float32)

    @pl.when(step == pl.num_programs(1) - 1)
    def _():
        per = sq_ref.shape[2]
        for block in range(sq_ref.shape[0]):
            flipped = jnp.transpose(squares[block * per : (block + 1) * per])
            row = jnp.sum(flipped, axis=0, keepdims=True)
            sq_ref[block] = jnp.broadcast_to(row, (8, per))


def project(slot, gathered, gain_here, w_query, w_pair, ctx_count):
    tokens_all = slot.shape[0]
    slots, columns = gathered.shape
    tok_here = tokens_all // ctx_count
    rows = min(tokens_all, 1024)
    tile = min(columns, 512)
    q_wide, p_wide = w_query.shape[1], w_pair.shape[1]
    return pl.pallas_call(
        project_kernel,
        grid=(tokens_all // rows, columns // tile),
        out_shape=[
            jax.ShapeDtypeStruct((tokens_all, q_wide), jnp.float32),
            jax.ShapeDtypeStruct((tokens_all, p_wide), jnp.float32),
            jax.ShapeDtypeStruct((ctx_count, 8, tok_here), jnp.float32),
        ],
        in_specs=[
            pl.BlockSpec((rows, 128), lambda i, j: (i, 0)),
            pl.BlockSpec((slots, tile), lambda i, j: (0, j)),
            pl.BlockSpec((1, tile), lambda i, j: (0, j)),
            pl.BlockSpec((tile, q_wide), lambda i, j: (j, 0)),
            pl.BlockSpec((tile, p_wide), lambda i, j: (j, 0)),
        ],
        out_specs=[
            pl.BlockSpec((rows, q_wide), lambda i, j: (i, 0)),
            pl.BlockSpec((rows, p_wide), lambda i, j: (i, 0)),
            pl.BlockSpec((rows // tok_here, 8, tok_here), lambda i, j: (i, 0, 0)),
        ],
        scratch_shapes=[
            pltpu.VMEM((rows, slots), jnp.bfloat16),
            pltpu.VMEM((rows, 128), jnp.float32),
        ],
        compiler_params=pltpu.CompilerParams(
            dimension_semantics=("arbitrary", "arbitrary"), vmem_limit_bytes=VMEM_LIMIT
        ),
    )(
        jnp.broadcast_to(slot[:, None], (tokens_all, 128)),
        gathered,
        gain_here.reshape(1, columns),
        w_query,
        w_pair,
    )


def fold_kernel(n, pieces, arrays, *refs):
    parts, outs = refs[:arrays], refs[arrays : 2 * arrays]
    near, far = refs[2 * arrays : 3 * arrays], refs[3 * arrays : 4 * arrays]
    near_send, near_recv, far_send, far_recv = refs[4 * arrays :]
    chips = n // 2
    me = lax.axis_index("ctx")
    chip, core = me // 2, lax.rem(me, 2)
    mate = chip * 2 + 1 - core
    remote = [lax.rem(chip + step, chips) * 2 + core for step in range(1, chips)]
    greet("ctx", [mate] + remote)
    sends = []

    def give(index, step):
        which, low, size = pieces[index]
        target = lax.rem(chip + step, chips) * 2 + 1 - core
        sent = pltpu.make_async_remote_copy(
            src_ref=parts[which].at[target, pl.ds(low, size)],
            dst_ref=near[which].at[step, pl.ds(low, size)],
            send_sem=near_send.at[index, step],
            recv_sem=near_recv.at[index, step],
            device_id={"ctx": mate},
            device_id_type=MESH,
        )
        sent.start()
        sends.append(sent)
        return sent

    handed = {}
    for step in list(range(1, chips)) + [0]:
        for index in range(len(pieces)):
            handed[index, step] = give(index, step)
    crossed = {}
    for index, (which, low, size) in enumerate(pieces):
        rows = pl.ds(low, size)
        for step in range(1, chips):
            target = remote[step - 1]
            handed[index, step].wait_recv()
            near[which][step, rows] = near[which][step, rows] + parts[which][target, rows]
            sent = pltpu.make_async_remote_copy(
                src_ref=near[which].at[step, rows],
                dst_ref=far[which].at[step, rows],
                send_sem=far_send.at[index, step],
                recv_sem=far_recv.at[index, step],
                device_id={"ctx": target},
                device_id_type=MESH,
            )
            sent.start()
            sends.append(sent)
            crossed[index, step] = sent
    for index, (which, low, size) in enumerate(pieces):
        rows = pl.ds(low, size)
        handed[index, 0].wait_recv()
        total = parts[which][me, rows] + near[which][0, rows]
        for step in range(1, chips):
            crossed[index, step].wait_recv()
            total = total + far[which][step, rows]
        outs[which][rows] = total
    for sent in sends:
        sent.wait_send()


def fold(*arrays):
    n = arrays[0].shape[0]
    chips = n // 2
    pieces = []
    for which, array in enumerate(arrays):
        size = array.shape[1]
        cut = size // 4 if size * array.shape[2] > 131072 else size
        pieces += [(which, low, cut) for low in range(0, size, cut)]
    sems = pltpu.SemaphoreType.DMA((len(pieces), chips))
    slots = [pltpu.VMEM((chips,) + a.shape[1:], a.dtype) for a in arrays]
    return pl.pallas_call(
        functools.partial(fold_kernel, n, tuple(pieces), len(arrays)),
        out_shape=[jax.ShapeDtypeStruct(a.shape[1:], a.dtype) for a in arrays],
        in_specs=[VMEM_SPEC] * len(arrays),
        out_specs=[VMEM_SPEC] * len(arrays),
        scratch_shapes=slots + slots + [sems] * 4,
        compiler_params=pltpu.CompilerParams(
            collective_id=2, has_side_effects=True, vmem_limit_bytes=VMEM_LIMIT
        ),
    )(*arrays)


def share_kernel(n, x_ref, out_ref, own_sem, send_sem, recv_sem):
    me = lax.axis_index("ctx")
    greet("ctx", [lax.rem(me + step, n) for step in range(1, n)])
    own = pltpu.make_async_copy(x_ref, out_ref.at[me], own_sem)
    own.start()
    copies = []
    for step in range(1, n):
        copy = pltpu.make_async_remote_copy(
            src_ref=x_ref,
            dst_ref=out_ref.at[me],
            send_sem=send_sem.at[step],
            recv_sem=recv_sem.at[step],
            device_id={"ctx": lax.rem(me + step, n)},
            device_id_type=MESH,
        )
        copy.start()
        copies.append(copy)
    for step in range(1, n):
        lands = out_ref.at[lax.rem(me + n - step, n)]
        pltpu.make_async_copy(lands, lands, recv_sem.at[step]).wait()
    own.wait()
    for copy in copies:
        copy.wait_send()


def share(rows):
    n = lax.axis_size("ctx")
    out = pl.pallas_call(
        functools.partial(share_kernel, n),
        out_shape=jax.ShapeDtypeStruct((n,) + rows.shape, rows.dtype),
        in_specs=[VMEM_SPEC],
        out_specs=VMEM_SPEC,
        scratch_shapes=[
            pltpu.SemaphoreType.DMA,
            pltpu.SemaphoreType.DMA((n,)),
            pltpu.SemaphoreType.DMA((n,)),
        ],
        compiler_params=pltpu.CompilerParams(collective_id=3, has_side_effects=True),
    )(rows)
    return out.reshape(n * rows.shape[0], rows.shape[1])


def rotary(values_in, pos_rows):
    half_dim = values_in.shape[-1] // 2
    steps_up = jnp.arange(half_dim, dtype=jnp.float32)
    freqs = jnp.power(rotary_base, -2.0 * steps_up / values_in.shape[-1])
    angle = pos_rows.astype(jnp.float32)[:, None] * freqs[None, :]
    angle = angle.reshape((angle.shape[0],) + (1,) * (values_in.ndim - 2) + (half_dim,))
    cosine = jnp.cos(angle)
    sine = jnp.sin(angle)
    first = values_in[..., :half_dim]
    second = values_in[..., half_dim:]
    return jnp.concatenate(
        [first * cosine - second * sine, second * cosine + first * sine], axis=-1
    )


def document_of(pos_rows, doc_lengths):
    ends = jnp.cumsum(doc_lengths)
    return jnp.sum((ends[None, :] <= pos_rows[:, None]).astype(jnp.int32), axis=1)


def plan(token_ids, vocab_here, capacity):
    tokens_all = token_ids.shape[0]
    order = jnp.arange(tokens_all, dtype=jnp.int32)
    same = token_ids[:, None] == token_ids[None, :]
    first = jnp.min(jnp.where(same, order[None, :], tokens_all), axis=1)
    shard = token_ids // vocab_here
    leads = first == order
    before = (order[None, :] < first[:, None]) & leads[None, :] & (shard[None, :] == shard[:, None])
    rank = jnp.sum(before.astype(jnp.int32), axis=1)
    most = jnp.max(rank) + 1
    return shard, rank, leads, (most + capacity - 1) // capacity


def shards(token_ids, doc_lengths, block_order, table, gain, w_query, w_keyval):
    ctx_count = lax.axis_size("ctx")
    ctx_at = lax.axis_index("ctx")
    tp_count = lax.axis_size("tp")
    tp_at = lax.axis_index("tp")
    tokens_all = token_ids.shape[0]
    tok_here = tokens_all // ctx_count
    vocab_here = table.shape[0]
    columns = table.shape[1]
    width = gain.shape[0]
    heads_here = HEADS // tp_count
    blocks = tokens_all // BLOCK
    capacity = tokens_all // tp_count
    positions = (
        block_order[:, None] * BLOCK + jnp.arange(BLOCK, dtype=jnp.int32)[None, :]
    ).reshape(tokens_all)

    def redeal(values):
        pick = block_order[:, None] == jnp.arange(blocks, dtype=jnp.int32)[None, :]
        spread_out = jnp.where(pick[:, :, None], values.reshape(1, blocks, BLOCK), 0)
        return jnp.sum(spread_out, axis=1).reshape(tokens_all)

    shard, rank, leads, rounds = plan(token_ids, vocab_here, capacity)
    local_ids = token_ids - tp_at * vocab_here
    mine = leads & (shard == tp_at)
    row_shard, row_rank = redeal(shard), redeal(rank)

    kv_head = tp_at * heads_here // (HEADS // KV_HEADS)
    w_pair = lax.dynamic_slice_in_dim(w_keyval, kv_head * HD, HD, 2).reshape(
        w_keyval.shape[0], 2 * HD
    )
    gain_here = lax.dynamic_slice_in_dim(gain, ctx_at * columns, columns)

    def one_round(number, collective_id):
        wanted = number * capacity + jnp.arange(capacity, dtype=jnp.int32)
        hit = mine[None, :] & (rank[None, :] == wanted[:, None])
        asked = jnp.sum(jnp.where(hit, local_ids[None, :], 0), axis=1)
        gathered = spread(pick_rows(table, asked), collective_id)
        in_round = (row_rank >= number * capacity) & (row_rank < (number + 1) * capacity)
        slot = jnp.where(in_round, row_shard * capacity + row_rank - number * capacity, -1)
        return tuple(project(slot, gathered, gain_here, w_query, w_pair, ctx_count))

    terms = tuple(one_round(0, 0))
    query_term, pair_term, square_term = lax.fori_loop(
        1, rounds, lambda i, held: jax.tree.map(jnp.add, held, one_round(i, 1)), terms
    )
    pair_raw, query_raw, sumsq = fold(
        pair_term.reshape(ctx_count, tok_here, 2 * HD),
        query_term.reshape(ctx_count, tok_here, heads_here * HD),
        square_term,
    )
    inverse = lax.rsqrt(sumsq[0] / width + 1e-05)
    my_pos = lax.dynamic_slice_in_dim(positions, ctx_at * tok_here, tok_here)
    query_rows = rotary(
        (query_raw * inverse[:, None]).reshape(tok_here, heads_here, HD), my_pos
    ).astype(jnp.bfloat16)
    key_rows = rotary(pair_raw[:, :HD] * inverse[:, None], my_pos).astype(jnp.bfloat16)
    value_rows = (pair_raw[:, HD:] * inverse[:, None]).astype(jnp.bfloat16)
    my_doc = document_of(my_pos, doc_lengths)
    stacked = jnp.transpose(query_rows, (1, 0, 2)).reshape(heads_here * tok_here, HD)
    query_pos = jnp.tile(my_pos, heads_here)
    query_doc = jnp.tile(my_doc, heads_here)
    inv_root = 1.0 / jnp.sqrt(jnp.float32(HD))
    shared = share(jnp.concatenate([key_rows, value_rows], axis=1))
    key_piece, value_piece = shared[:, :HD], shared[:, HD:]
    key_doc = document_of(positions, doc_lengths)
    allowed = (key_doc[None, :] == query_doc[:, None]) & (positions[None, :] <= query_pos[:, None])
    scores = (
        lax.dot_general(
            stacked, key_piece, (((1,), (1,)), ((), ())), preferred_element_type=jnp.float32
        )
        * inv_root
    )
    masked = jnp.where(allowed, scores, jnp.float32(-1e30))
    largest = jnp.max(masked, axis=1)
    weights = jnp.where(allowed, jnp.exp(masked - largest[:, None]), jnp.float32(0.0))
    totals = jnp.sum(weights, axis=1)
    accum = jnp.dot(weights.astype(jnp.bfloat16), value_piece, preferred_element_type=jnp.float32)
    mixed = (accum / totals[:, None]).reshape(heads_here, tok_here, HD)
    return jnp.transpose(mixed, (1, 0, 2)).reshape(tok_here, heads_here * HD).astype(jnp.bfloat16)


def solution(mesh):
    in_specs = (P(), P(), P(), P("tp", "ctx"), P(), P("ctx", "tp"), P("ctx", None, None))
    out_specs = P("ctx", "tp")
    return jax.shard_map(shards, mesh=mesh, in_specs=in_specs, out_specs=out_specs, check_vma=False)
```
